32 devices in a mesh: req: 16 (over z, y, x), tp: 2 (over core).
Axes of the slice: x: 2, y: 2, z: 4, core: 2. Of those that a mesh axis runs over, the one named last changes fastest.
Arguments:
- tokens: bfloat16 [8192, 5120], P(('req', 'tp')), may hold values from -200 to 200
- norm_gain: float32 [5120], replicated, may hold values from 0.1 to 1.9
- w_query: bfloat16 [5120, 3072], P('req', 'tp'), may hold values from -0.078125 to 0.078125
- w_kv: bfloat16 [5120, 2, 1024], P('req', None, 'tp'), may hold values from -0.078125 to 0.078125
- q_gain: float32 [128], replicated, may hold values from 0.5 to 60, as said below
- k_gain: float32 [128], replicated, may hold values from 0.1 to 1.9
- seg_ids: int32 [16, 512], P('req'), may hold values from 0 to 5, never falling along the last dimension, each value on 1 to 256 neighbouring positions
- page_table: int32 [16, 8], replicated, may hold values from 0 to 127, as said below
Outputs:
- attended: bfloat16 [8192, 3072], P('req', 'tp')
- cache: bfloat16 [16, 8, 64, 2, 1024], P('req', None, None, None, 'tp')
The draws below stay inside these ranges and needn't reach their ends.
Inputs may be any that keep to these rules, and one draw needn't show every extreme that they name: page_table[r, p] = o * 8 + s sends page p of pack r to slot s of owner o; every slot of every owner receives exactly one page, and the pages of one pack go to different owners. `seg_ids`: nondecreasing along each pack; every pack holds 6 prompts. `q_gain`: positive.
All inputs are finite; a program needn't handle non-finite values.
Results may differ from the reference program's by a relative error of at most 0.008.
The reference program's roundings to bfloat16 on the way count: a program that leaves them out, or rounds other values in their place, can miss the bound.
Values may be sent and summed in bfloat16 or wider, within the bound.
A program may use at most 128 MiB of HBM per device.

```python
import math
import jax
import jax.numpy as jnp
import numpy as np
from jax import lax

D = 5120
HD = 128
QH = 24
KVH = 8
SEGS = 6
T_REQ = 512
PAGE = 64
P_DEV = 8
TOKENS = 8192
N_REQ = 16


def draw_tokens(key, part):
    first, second, third = jax.random.split(key, 3)
    base = jax.random.normal(first, (TOKENS, D), jnp.float32)
    row_scale = jnp.exp(jax.random.uniform(second, (TOKENS, 1), jnp.float32, 0.0, 2.3))
    col_scale = jnp.exp(jax.random.uniform(third, (1, D), jnp.float32, 0.0, 2.3))
    return jnp.clip(base * row_scale * col_scale / 3.0, -200.0, 200.0).astype(jnp.bfloat16)


def draw_q_gain(key, part):
    low, high = (math.log(0.5), math.log(2.0))
    spread = jax.random.uniform(key, (HD,), jnp.float32)
    return jnp.exp(low + spread * (high - low))


def draw_page_table(key, part):
    packs = TOKENS // T_REQ
    first, second, third = jax.random.split(jax.random.fold_in(key, 7), 3)
    order = jax.random.permutation(first, packs).astype(jnp.int32)
    rank = jnp.argsort(order, stable=True).astype(jnp.int32)
    offsets = jax.random.permutation(second, packs).astype(jnp.int32)[:P_DEV]
    turn = jax.random.randint(third, (packs,), 0, P_DEV).astype(jnp.int32)
    owners = order[(rank[:, None] + offsets[None, :]) % packs]
    slots = (jnp.arange(P_DEV, dtype=jnp.int32)[None, :] + turn[owners]) % P_DEV
    return (owners * P_DEV + slots).astype(jnp.int32)


def level_of(own_key, extent, pieces, least, largest):
    def one(position, shards_of):
        steps = jax.random.uniform(jax.random.fold_in(jax.random.fold_in(own_key, 6), position), (shards_of,), jnp.float32, least / len(pieces), largest / len(pieces))
        return jnp.repeat(jnp.exp(steps), extent[position] // shards_of).reshape((-1,) + (1,) * (len(extent) - position - 1))

    loudness = one(*pieces[0])
    for cut in pieces[1:]:
        loudness = loudness * one(*cut)
    return loudness


def length_profile(count, total, limit, skew):
    portions = [(1 << 20) // math.isqrt(standing ** skew) + 1 for standing in range(2, count + 1)]
    surplus, holding = total - limit - (count - 1), [1] * (count - 1)
    while surplus > 0:
        movable = [i for i in range(count - 1) if holding[i] < limit]
        whole, left = sum([portions[i] for i in movable]), surplus
        for i in movable:
            addition = min(limit - holding[i], max(1, left * portions[i] // whole), surplus)
            holding[i] = holding[i] + addition
            surplus = surplus - addition
    return np.array([limit] + holding)


def ragged_sizes(rng, amount, total, limit, slope):
    if amount == 2:
        one = jax.random.randint(rng, (), max(1, total - limit), min(limit, total - 1) + 1)
        return jnp.stack([one, total - one])
    sizes = jnp.asarray(length_profile(amount, total, limit, slope), jnp.int32)
    pairs = (amount - 1) // 2
    giver, receiver = sizes[1:1 + 2 * pairs:2], sizes[2:2 + 2 * pairs:2]
    margin = jnp.minimum(giver - 1, limit - receiver)
    shifted = jax.random.randint(jax.random.fold_in(rng, 1), (pairs,), 0, 1 << 20) % (margin + 1)
    sizes = sizes.at[1:1 + 2 * pairs:2].set(giver - shifted).at[2:2 + 2 * pairs:2].set(receiver + shifted)
    return sizes[jax.random.permutation(jax.random.fold_in(rng, 2), amount)]


def normal_values(own_key, dims, scale, bound, pieces=(), kind=jnp.bfloat16):
    entries = scale * jax.random.normal(own_key, dims, jnp.float32)
    if pieces:
        entries = entries * level_of(own_key, dims, pieces, -0.22, 0.18)
    return jnp.clip(entries, -bound, bound).astype(kind)


def setup_inputs(seed: int = 0) -> dict:
    seeds = jax.random.split(jax.random.key(seed), 9)
    return {
        "tokens": draw_tokens(jax.random.fold_in(seeds[8], 71), 0),
        "norm_gain": jnp.clip(1.0 + 0.18 * jax.random.normal(seeds[1], (D,), jnp.float32), 0.1, 1.9),
        "w_query": normal_values(seeds[2], (D, QH * HD), D ** -0.5, 0.078125, ((0, 16), (1, 2))),
        "w_kv": normal_values(seeds[3], (D, 2, KVH * HD), D ** -0.5, 0.078125, ((0, 16), (2, 2))),
        "q_gain": draw_q_gain(jax.random.fold_in(seeds[8], 71), 0),
        "k_gain": jnp.clip(1.0 + 0.18 * jax.random.normal(seeds[5], (HD,), jnp.float32), 0.1, 1.9),
        "seg_ids": jax.vmap(lambda own: jnp.searchsorted(jnp.cumsum(ragged_sizes(own, SEGS, T_REQ, T_REQ // 2, 2)), jnp.arange(T_REQ), side="right"))(jax.random.split(seeds[6], N_REQ)).reshape((N_REQ, T_REQ)).astype(jnp.int32),
        "page_table": draw_page_table(jax.random.fold_in(seeds[8], 71), 0),
    }


def rope_tables(positions, width):
    half = width // 2
    freqs = jnp.power(jnp.float32(1000000.0), -jnp.arange(half, dtype=jnp.float32) * 2.0 / width)
    angles = positions.astype(jnp.float32)[:, None] * freqs[None, :]
    angles = jnp.concatenate([angles, angles], axis=1)
    return (jnp.cos(angles), jnp.sin(angles))

def head_norm_rope(values, gain, cosine, sine):
    scaled = values * lax.rsqrt(lax.optimization_barrier(jnp.mean(values * values, axis=-1, keepdims=True)) + 1e-06) * gain
    half = values.shape[-1] // 2
    turned = jnp.concatenate([-scaled[..., half:], scaled[..., :half]], axis=-1)
    return (scaled * cosine[:, None, :] + turned * sine[:, None, :]).astype(jnp.bfloat16)

def segment_positions(seg_row):
    before = lax.optimization_barrier(jnp.sum((seg_row[None, :] < seg_row[:, None]).astype(jnp.int32), axis=1))
    return jnp.arange(seg_row.shape[0], dtype=jnp.int32) - before

def one_pack(tokens, seg_row, norm_gain, w_query, w_kv, q_gain, k_gain):
    values_in = tokens.astype(jnp.float32)
    normed = (values_in * lax.rsqrt(lax.optimization_barrier(jnp.mean(values_in * values_in, axis=1, keepdims=True)) + 1e-06) * norm_gain).astype(jnp.bfloat16)
    query = jnp.dot(normed, w_query, preferred_element_type=jnp.float32)
    keyval = jnp.dot(normed, w_kv.reshape(w_kv.shape[0], -1), preferred_element_type=jnp.float32)
    keyval = keyval.reshape(T_REQ, 2, KVH, HD)
    positions = segment_positions(seg_row)
    cosine, sine = rope_tables(positions, HD)
    q_normed = head_norm_rope(query.reshape(T_REQ, QH, HD), q_gain, cosine, sine)
    k_normed = head_norm_rope(keyval[:, 0], k_gain, cosine, sine)
    v_round = keyval[:, 1].astype(jnp.bfloat16)
    group = QH // KVH
    keys_wide = jnp.repeat(k_normed, group, axis=1).astype(jnp.float32)
    values_wide = jnp.repeat(v_round, group, axis=1).astype(jnp.float32)
    scores = jnp.einsum('qhd,khd->hqk', q_normed.astype(jnp.float32), keys_wide) * HD ** (-0.5)
    index = jnp.arange(T_REQ, dtype=jnp.int32)
    allowed = (seg_row[:, None] == seg_row[None, :]) & (index[None, :] <= index[:, None])
    scores = jnp.where(allowed[None], scores, -1e+30)
    probs = jax.nn.softmax(scores, axis=-1).astype(jnp.bfloat16)
    attended = jnp.einsum('hqk,khd->qhd', probs.astype(jnp.float32), values_wide)
    attended = attended.reshape(T_REQ, QH * HD).astype(jnp.bfloat16)
    pages = jnp.stack([k_normed, v_round], axis=1).reshape(P_DEV, PAGE, 2, KVH * HD)
    return (attended, pages)

def reference(tokens, norm_gain, w_query, w_kv, q_gain, k_gain, seg_ids, page_table):

    def step(packed):
        return one_pack(packed[0], packed[1], norm_gain, w_query, w_kv, q_gain, k_gain)
    attended, pages = lax.map(step, (tokens.reshape(N_REQ, T_REQ, D), seg_ids))
    attended = attended.reshape(TOKENS, QH * HD)
    pages = pages.reshape(N_REQ * P_DEV, PAGE, 2, KVH * HD)
    cache = jnp.zeros_like(pages).at[page_table.reshape(-1)].set(pages)
    return (attended, cache.reshape(N_REQ, P_DEV, PAGE, 2, KVH * HD))
```

```python
import functools

import jax
import jax.numpy as jnp
from jax import lax
from jax.experimental import pallas as pl
from jax.experimental.pallas import tpu as pltpu
from jax.sharding import PartitionSpec as P

HD = 128


def rope_tables(positions, width):
    half = width // 2
    freqs = jnp.power(jnp.float32(1000000.0), -jnp.arange(half, dtype=jnp.float32) * 2.0 / width)
    angles = positions.astype(jnp.float32)[:, None] * freqs[None, :]
    angles = jnp.concatenate([angles, angles], axis=1)
    return (jnp.cos(angles), jnp.sin(angles))


def head_norm_rope(values, gain, cosine, sine):
    scaled = values * lax.rsqrt(jnp.mean(values * values, axis=-1, keepdims=True) + 1e-06) * gain
    half = values.shape[-1] // 2
    turned = jnp.concatenate([-scaled[..., half:], scaled[..., :half]], axis=-1)
    return (scaled * cosine[:, None, :] + turned * sine[:, None, :]).astype(jnp.bfloat16)


def segment_positions(seg_row):
    before = jnp.sum((seg_row[None, :] < seg_row[:, None]).astype(jnp.int32), axis=1)
    return jnp.arange(seg_row.shape[0], dtype=jnp.int32) - before


def body(tokens, norm_gain, w_query, w_kv, q_gain, k_gain, seg_ids, page_table):
    values_in = tokens.astype(jnp.float32)
    normed = (
        values_in
        * lax.rsqrt(jnp.mean(values_in * values_in, axis=1, keepdims=True) + 1e-06)
        * norm_gain
    ).astype(jnp.bfloat16)
    query_width = w_query.shape[1]
    kv_flat = w_kv.reshape(w_kv.shape[0], -1)
    whole = lax.all_gather(normed, "tp", axis=0, tiled=True)
    query = jnp.dot(
        whole,
        lax.all_gather(w_query, "req", axis=0, tiled=True),
        preferred_element_type=jnp.float32,
    )
    keyval = jnp.dot(
        whole,
        lax.all_gather(kv_flat, "req", axis=0, tiled=True),
        preferred_element_type=jnp.float32,
    )
    count = query.shape[0]
    local_heads = query_width // HD
    local_kv = kv_flat.shape[1] // (2 * HD)
    group = local_heads // local_kv
    seg_row = seg_ids[0]
    positions = segment_positions(seg_row)
    cosine, sine = rope_tables(positions, HD)
    q_normed = head_norm_rope(query.reshape(count, local_heads, HD), q_gain, cosine, sine)
    keyval = keyval.reshape(count, 2, local_kv, HD)
    k_normed = head_norm_rope(keyval[:, 0], k_gain, cosine, sine)
    v_round = keyval[:, 1].astype(jnp.bfloat16)
    pages_dev = page_table.shape[1]
    page_len = count // pages_dev
    devices = lax.axis_size("req")
    me = lax.axis_index("req")
    stacked = jnp.stack([k_normed, v_round], axis=1).reshape(
        pages_dev, page_len * 2 * local_kv * HD
    )
    my_row = lax.dynamic_slice_in_dim(page_table, me, 1, 0)[0]
    owners = my_row // pages_dev
    send_map = (owners[None, :] == jnp.arange(devices, dtype=jnp.int32)[:, None]).astype(
        jnp.bfloat16
    )
    outgoing = jnp.dot(send_map, stacked, preferred_element_type=jnp.float32).astype(jnp.bfloat16)
    incoming = lax.all_to_all(outgoing, "req", split_axis=0, concat_axis=0, tiled=True)
    targets = me * pages_dev + jnp.arange(pages_dev, dtype=jnp.int32)
    recv_map = jnp.any(page_table[None, :, :] == targets[:, None, None], axis=2).astype(
        jnp.bfloat16
    )
    cache = jnp.dot(recv_map, incoming, preferred_element_type=jnp.float32).astype(jnp.bfloat16)
    cache = cache.reshape(1, pages_dev, page_len, 2, local_kv * HD)
    grouped_q = q_normed.reshape(count, local_kv, group, HD)
    scale = HD ** (-0.5)
    index = jnp.arange(count, dtype=jnp.int32)
    scores = (
        jnp.einsum("qcgd,kcd->cgqk", grouped_q, k_normed, preferred_element_type=jnp.float32)
        * scale
    )
    allowed = (seg_row[:, None] == seg_row[None, :]) & (index[None, :] <= index[:, None])
    scores = jnp.where(allowed[None, None], scores, -1e30)
    probs = jax.nn.softmax(scores, axis=-1).astype(jnp.bfloat16)
    attended = jnp.einsum("cgqk,kcd->qcgd", probs, v_round, preferred_element_type=jnp.float32)
    attended = attended.reshape(count, local_heads * HD).astype(jnp.bfloat16)
    return (attended, cache)


MESH = pl.DeviceIdType.MESH
SIDE = 2
PLANE = SIDE * SIDE
PARTS = 4


def place():
    me = lax.axis_index("req")
    core = lax.axis_index("tp")
    z = me // PLANE
    q = me % PLANE
    across = q + 1 - 2 * (q % SIDE)
    along = (q + SIDE) % PLANE
    diagonal = PLANE - 1 - q
    return me, core, z, q, across, along, diagonal


def gather_kernel(depth, x_ref, w_ref, seg_ref, xs_ref, ws_ref, segs_ref,
                  xbuf, wbuf, sbuf, own_sem, w_send, w_recv, up_send, up_recv, down_send, down_recv,
                  x_send, x_recv, hop_send, hop_recv, near_send, near_recv, s_send, s_recv):
    me, core, z, q, across, along, diagonal = place()
    base = z * PLANE
    mates = (across, along, diagonal)
    barrier = pltpu.get_barrier_semaphore()
    for mate in mates:
        pl.semaphore_signal(barrier, inc=1, device_id=(base + mate, core), device_id_type=MESH)
    pl.semaphore_signal(barrier, inc=1, device_id=(me, 1 - core), device_id_type=MESH)

    @pl.when(z > 0)
    def _():
        pl.semaphore_signal(barrier, inc=1, device_id=(me - PLANE, core), device_id_type=MESH)

    @pl.when(z < depth - 1)
    def _():
        pl.semaphore_signal(barrier, inc=1, device_id=(me + PLANE, core), device_id_type=MESH)

    load_w = pltpu.make_async_copy(w_ref.at[q], wbuf, own_sem.at[0])
    load_x = pltpu.make_async_copy(x_ref, xbuf, own_sem.at[1])
    load_s = pltpu.make_async_copy(seg_ref, sbuf, own_sem.at[2])
    load_w.start()
    load_x.start()
    load_s.start()
    pl.semaphore_wait(barrier, len(mates) + 1 + (z > 0).astype(jnp.int32) + (z < depth - 1).astype(jnp.int32))
    rows = x_ref.shape[0] // PARTS

    def remote(source, target, send, receive, device):
        return pltpu.make_async_remote_copy(
            src_ref=source, dst_ref=target, send_sem=send, recv_sem=receive,
            device_id=device, device_id_type=MESH)

    def w_out(i):
        return remote(w_ref.at[mates[i]], ws_ref.at[z, q], w_send.at[i], w_recv.at[i], (base + mates[i], core))

    def w_in(i):
        return remote(w_ref.at[mates[i]], ws_ref.at[z, mates[i]], w_send.at[i], w_recv.at[i], (base + mates[i], core))

    def up(d, i, order):
        block = ws_ref.at[jnp.maximum(z - d, 0), order[i]]
        return remote(block, block, up_send.at[d, i], up_recv.at[d, i], (jnp.minimum(me + PLANE, depth * PLANE - 1), core))

    def down(d, i, order):
        block = ws_ref.at[jnp.minimum(z + d, depth - 1), order[i]]
        return remote(block, block, down_send.at[d, i], down_recv.at[d, i], (jnp.maximum(me - PLANE, 0), core))

    order = (q,) + mates

    def piece(owner, lane, k):
        return xs_ref.at[owner, lane, pl.ds(k * rows, rows)]

    def x_out(i, k):
        return remote(x_ref.at[pl.ds(k * rows, rows)], piece(q, core, k), x_send.at[i, k], x_recv.at[i, k], (base + mates[i], core))

    def x_in(i, k):
        return remote(x_ref.at[pl.ds(k * rows, rows)], piece(mates[i], core, k), x_send.at[i, k], x_recv.at[i, k], (base + mates[i], core))

    def hop(owner, k, target):
        return remote(piece(owner, core, k), piece(owner, core, k), hop_send.at[k], hop_recv.at[k], (base + target, core))

    def near(i, k):
        source = x_ref.at[pl.ds(k * rows, rows)] if i == 0 else piece(order[i], core, k)
        return remote(source, piece(order[i], core, k), near_send.at[i, k], near_recv.at[i, k], (me, 1 - core))

    def near_in(i, k):
        block = piece(order[i], 1 - core, k)
        return remote(block, block, near_send.at[i, k], near_recv.at[i, k], (me, 1 - core))

    def s_out(i):
        return remote(seg_ref, segs_ref.at[q], s_send.at[i], s_recv.at[i], (base + mates[i], core))

    def s_in(i):
        return remote(seg_ref, segs_ref.at[mates[i]], s_send.at[i], s_recv.at[i], (base + mates[i], core))

    for i in (2, 0, 1):
        w_out(i).start()
    for i in range(3):
        s_out(i).start()
    for k in range(PARTS):
        x_out(0, k).start()
        x_out(1, k).start()
    load_w.wait()
    save_w = pltpu.make_async_copy(wbuf, ws_ref.at[z, q], own_sem.at[0])
    save_w.start()
    load_s.wait()
    save_s = pltpu.make_async_copy(sbuf, segs_ref.at[q], own_sem.at[2])
    save_s.start()
    load_x.wait()
    save_x = pltpu.make_async_copy(xbuf, xs_ref.at[q, core], own_sem.at[1])
    save_x.start()
    save_w.wait()

    def push(d, i):
        @pl.when((z < depth - 1) & (z >= d))
        def _():
            up(d, i, order).start()

        @pl.when((z > 0) & (z + d < depth))
        def _():
            down(d, i, order).start()

    def arrive_up(d, i):
        block = ws_ref.at[jnp.maximum(z - d, 0), order[i]]
        remote(block, block, up_send.at[d - 1, i], up_recv.at[d - 1, i], (jnp.maximum(me - PLANE, 0), core)).wait_recv()

    def arrive_down(d, i):
        block = ws_ref.at[jnp.minimum(z + d, depth - 1), order[i]]
        remote(block, block, down_send.at[d - 1, i], down_recv.at[d - 1, i], (jnp.minimum(me + PLANE, depth * PLANE - 1), core)).wait_recv()

    def advance(d, i):
        @pl.when(z >= d)
        def _():
            arrive_up(d, i)
            if d < depth - 1:
                @pl.when(z < depth - 1)
                def _():
                    up(d, i, order).start()

        @pl.when(z + d < depth)
        def _():
            arrive_down(d, i)
            if d < depth - 1:
                @pl.when(z > 0)
                def _():
                    down(d, i, order).start()

    push(0, 0)
    for k in range(PARTS):
        near(0, k).start()
    for i in (0, 1, 2):
        w_in(i).wait_recv()
        push(0, i + 1)
    for k in range(PARTS):
        x_in(0, k).wait_recv()

        @pl.when(core == 0)
        def _():
            hop(across, k, along).start()

        near(1, k).start()
        x_in(1, k).wait_recv()

        @pl.when(core == 1)
        def _():
            hop(along, k, across).start()

        near(2, k).start()
        advance(1, k)
    for k in range(PARTS):
        advance(2, k)
        hop(diagonal, k, along).wait_recv()
        near(3, k).start()
    for i in range(PLANE):
        for d in range(3, depth):
            advance(d, i)
    for k in range(PARTS):
        for i in range(PLANE):
            near_in(i, k).wait_recv()
    for i in range(3):
        s_in(i).wait_recv()
        s_out(i).wait_send()
        w_out(i).wait_send()
    for k in range(PARTS):
        x_out(0, k).wait_send()
        x_out(1, k).wait_send()
        hop(across, k, along).wait_send()
        for i in range(PLANE):
            near(i, k).wait_send()
    for d in range(depth - 1):
        for i in range(PLANE):
            @pl.when((z < depth - 1) & (z >= d))
            def _():
                up(d, i, order).wait_send()

            @pl.when((z > 0) & (z + d < depth))
            def _():
                down(d, i, order).wait_send()
    save_x.wait()
    save_s.wait()


def gather(normed, blocks, seg, depth):
    rows, width = normed.shape
    dma = pltpu.SemaphoreType.DMA
    return pl.pallas_call(
        functools.partial(gather_kernel, depth),
        out_shape=(
            jax.ShapeDtypeStruct((PLANE, 2, rows, width), normed.dtype),
            jax.ShapeDtypeStruct((depth,) + blocks.shape, blocks.dtype),
            jax.ShapeDtypeStruct((PLANE,) + seg.shape, seg.dtype),
        ),
        in_specs=[pl.BlockSpec(memory_space=pl.ANY)] * 3,
        out_specs=(pl.BlockSpec(memory_space=pl.ANY),) * 3,
        scratch_shapes=[
            pltpu.VMEM(normed.shape, normed.dtype),
            pltpu.VMEM(blocks.shape[1:], blocks.dtype),
            pltpu.VMEM(seg.shape, seg.dtype),
            dma((3,)), dma((3,)), dma((3,)),
            dma((depth - 1, PLANE)), dma((depth - 1, PLANE)), dma((depth - 1, PLANE)), dma((depth - 1, PLANE)),
            dma((2, PARTS)), dma((2, PARTS)), dma((PARTS,)), dma((PARTS,)),
            dma((PLANE, PARTS)), dma((PLANE, PARTS)), dma((3,)), dma((3,)),
        ],
        compiler_params=pltpu.CompilerParams(collective_id=0, has_side_effects=True),
    )(normed, blocks, seg)


def return_kernel(total, att_ref, page_ref, out_ref, in_ref, abuf, pbuf, own_sem, a_send, a_recv, p_send, p_recv):
    me, core, z, q, across, along, diagonal = place()
    base = z * PLANE
    mates = (across, along, diagonal)
    barrier = pltpu.get_barrier_semaphore()
    for d in range(1, total):
        pl.semaphore_signal(barrier, inc=1, device_id=((me + d) % total, core), device_id_type=MESH)
    load_a = pltpu.make_async_copy(att_ref.at[q], abuf, own_sem.at[0])
    load_p = pltpu.make_async_copy(page_ref.at[me], pbuf, own_sem.at[1])
    load_a.start()
    load_p.start()
    pl.semaphore_wait(barrier, total - 1)
    width = att_ref.shape[2]

    def columns(owner):
        return out_ref.at[:, pl.ds(pl.multiple_of(owner * width, 128), width)]

    def a_copy(i, owner):
        return pltpu.make_async_remote_copy(
            src_ref=att_ref.at[mates[i]], dst_ref=columns(owner), send_sem=a_send.at[i], recv_sem=a_recv.at[i],
            device_id=(base + mates[i], core), device_id_type=MESH)

    def p_copy(d, slot, target):
        return pltpu.make_async_remote_copy(
            src_ref=page_ref.at[target], dst_ref=in_ref.at[slot], send_sem=p_send.at[d - 1], recv_sem=p_recv.at[d - 1],
            device_id=(target, core), device_id_type=MESH)

    far = [d for d in range(1, total)]
    for d in far:
        p_copy(d, me, (me + d) % total).start()
    for i in (2, 0, 1):
        a_copy(i, q).start()
    load_a.wait()
    load_p.wait()
    save_a = pltpu.make_async_copy(abuf, columns(q), own_sem.at[0])
    save_p = pltpu.make_async_copy(pbuf, in_ref.at[me], own_sem.at[1])
    save_a.start()
    save_p.start()
    for i in range(3):
        a_copy(i, mates[i]).wait_recv()
        a_copy(i, q).wait_send()
    for d in far:
        p_copy(d, (me + total - d) % total, (me + d) % total).wait_recv()
        p_copy(d, me, (me + d) % total).wait_send()
    save_a.wait()
    save_p.wait()


def give_back(attended, pages):
    total = pages.shape[0]
    dma = pltpu.SemaphoreType.DMA
    packs, count, width = attended.shape
    return pl.pallas_call(
        functools.partial(return_kernel, total),
        out_shape=(
            jax.ShapeDtypeStruct((count, packs * width), attended.dtype),
            jax.ShapeDtypeStruct(pages.shape, pages.dtype),
        ),
        in_specs=[pl.BlockSpec(memory_space=pl.ANY)] * 2,
        out_specs=(pl.BlockSpec(memory_space=pl.ANY),) * 2,
        scratch_shapes=[
            pltpu.VMEM(attended.shape[1:], attended.dtype),
            pltpu.VMEM(pages.shape[1:], pages.dtype),
            dma((2,)), dma((3,)), dma((3,)), dma((total - 1,)), dma((total - 1,)),
        ],
        compiler_params=pltpu.CompilerParams(collective_id=1, has_side_effects=True),
    )(attended, pages)


def pick_kernel(index_ref, kv_ref, out_ref):
    owners, packs = out_ref.shape[0], out_ref.shape[1]

    def one(step, carry):
        o, p = step // packs, step % packs
        out_ref[o, p] = kv_ref[p, index_ref[o, p]]
        return carry

    lax.fori_loop(0, owners * packs, one, 0)


def pick_pages(index, kv):
    packs, pages, rows, width = kv.shape
    return pl.pallas_call(
        pick_kernel,
        out_shape=jax.ShapeDtypeStruct((index.shape[0], packs, rows, width), kv.dtype),
        in_specs=[pl.BlockSpec(memory_space=pltpu.SMEM), pl.BlockSpec(memory_space=pltpu.VMEM)],
        out_specs=pl.BlockSpec(memory_space=pltpu.VMEM),
    )(index, kv)


def plane_body(tokens, norm_gain, w_query, w_kv, q_gain, k_gain, seg_ids, page_table):
    me = lax.axis_index("req")
    devices = lax.axis_size("req")
    depth = devices // PLANE
    z = me // PLANE
    values_in = tokens.astype(jnp.float32)
    normed = (
        values_in
        * lax.rsqrt(jnp.mean(values_in * values_in, axis=1, keepdims=True) + 1e-06)
        * norm_gain
    ).astype(jnp.bfloat16)
    inner = w_query.shape[0]
    q_width = w_query.shape[1] // PLANE
    group = q_width // HD
    blocks = jnp.concatenate(
        [
            w_query.reshape(inner, PLANE, q_width),
            w_kv[:, 0].reshape(inner, PLANE, HD),
            w_kv[:, 1].reshape(inner, PLANE, HD),
        ],
        axis=2,
    ).transpose(1, 0, 2)
    count = seg_ids.shape[1]
    xs, ws, segs = gather(normed, blocks, seg_ids.reshape(-1, HD), depth)
    everything = jnp.dot(
        xs.reshape(PLANE * count, -1),
        ws.reshape(devices * inner, -1),
        preferred_element_type=jnp.float32,
    )
    seg = segs.reshape(PLANE, count)
    positions = jax.vmap(segment_positions)(seg)
    cosine, sine = rope_tables(positions.reshape(-1), HD)
    q_normed = head_norm_rope(everything[:, :q_width].reshape(-1, group, HD), q_gain, cosine, sine)
    k_normed = head_norm_rope(everything[:, None, q_width : q_width + HD], k_gain, cosine, sine)[:, 0]
    v_round = everything[:, q_width + HD :].astype(jnp.bfloat16)
    pages_dev = page_table.shape[1]
    page_len = count // pages_dev
    kv = jnp.concatenate([k_normed, v_round], axis=1).reshape(PLANE, pages_dev, page_len, 2 * HD)
    rows = lax.dynamic_slice_in_dim(page_table, z * PLANE, PLANE, 0) // pages_dev
    match = rows[None, :, :] == jnp.arange(devices, dtype=jnp.int32)[:, None, None]
    index = jnp.sum(match * jnp.arange(pages_dev, dtype=jnp.int32), axis=2)
    outgoing = pick_pages(index, kv)
    scale = HD ** (-0.5)
    order = jnp.arange(count, dtype=jnp.int32)
    scores = (
        jnp.einsum(
            "pqgd,pkd->pgqk",
            q_normed.reshape(PLANE, count, group, HD),
            k_normed.reshape(PLANE, count, HD),
            preferred_element_type=jnp.float32,
        )
        * scale
    )
    allowed = (seg[:, :, None] == seg[:, None, :]) & (order[None, None, :] <= order[None, :, None])
    scores = jnp.where(allowed[:, None], scores, -1e30)
    probs = jax.nn.softmax(scores, axis=-1).astype(jnp.bfloat16)
    attended = jnp.einsum(
        "pgqk,pkd->pqgd", probs, v_round.reshape(PLANE, count, HD), preferred_element_type=jnp.float32
    )
    attended = attended.reshape(PLANE, count, q_width).astype(jnp.bfloat16)
    attended, incoming = give_back(attended, outgoing)
    targets = me * pages_dev + jnp.arange(pages_dev, dtype=jnp.int32)
    found = jnp.any(page_table[None, :, :] == targets[:, None, None], axis=2)
    source = jnp.sum(found * jnp.arange(devices, dtype=jnp.int32), axis=1)
    cache = collect(source, incoming)
    return (attended, cache[None])


def collect_kernel(source_ref, in_ref, out_ref):
    slots = out_ref.shape[0]
    for s in range(slots):
        r = source_ref[s]
        for h in range(PLANE):
            page = in_ref[(r // PLANE) * PLANE + h, r % PLANE]
            for half in range(2):
                out_ref[s, :, half, h * HD : (h + 1) * HD] = page[:, half * HD : (half + 1) * HD]


def collect(source, incoming):
    slots = source.shape[0]
    rows = incoming.shape[2]
    return pl.pallas_call(
        collect_kernel,
        out_shape=jax.ShapeDtypeStruct((slots, rows, 2, PLANE * HD), incoming.dtype),
        in_specs=[pl.BlockSpec(memory_space=pltpu.SMEM), pl.BlockSpec(memory_space=pltpu.VMEM)],
        out_specs=pl.BlockSpec(memory_space=pltpu.VMEM),
    )(source, incoming)


def solution(mesh):
    placed = (
        P(("req", "tp"), None),
        P(),
        P("req", "tp"),
        P("req", None, "tp"),
        P(),
        P(),
        P("req", None),
        P(),
    )
    planes = mesh.shape["req"] == 4 * PLANE and mesh.shape["tp"] == 2
    return jax.shard_map(
        plane_body if planes else body,
        mesh=mesh,
        in_specs=placed,
        out_specs=(P("req", "tp"), P("req", None, None, None, "tp")),
        check_vma=False,
    )
```

```python
import functools

import jax
import jax.numpy as jnp
from jax import lax
from jax.experimental import pallas as pl
from jax.experimental.pallas import tpu as pltpu
from jax.sharding import PartitionSpec as P

HD = 128


def rope_tables(positions, width):
    half = width // 2
    freqs = jnp.power(jnp.float32(1000000.0), -jnp.arange(half, dtype=jnp.float32) * 2.0 / width)
    angles = positions.astype(jnp.float32)[:, None] * freqs[None, :]
    angles = jnp.concatenate([angles, angles], axis=1)
    return (jnp.cos(angles), jnp.sin(angles))


def head_norm_rope(values, gain, cosine, sine):
    scaled = values * lax.rsqrt(jnp.mean(values * values, axis=-1, keepdims=True) + 1e-06) * gain
    half = values.shape[-1] // 2
    turned = jnp.concatenate([-scaled[..., half:], scaled[..., :half]], axis=-1)
    return (scaled * cosine[:, None, :] + turned * sine[:, None, :]).astype(jnp.bfloat16)


def segment_positions(seg_row):
    before = jnp.sum((seg_row[None, :] < seg_row[:, None]).astype(jnp.int32), axis=1)
    return jnp.arange(seg_row.shape[0], dtype=jnp.int32) - before


def body(tokens, norm_gain, w_query, w_kv, q_gain, k_gain, seg_ids, page_table):
    values_in = tokens.astype(jnp.float32)
    normed = (
        values_in
        * lax.rsqrt(jnp.mean(values_in * values_in, axis=1, keepdims=True) + 1e-06)
        * norm_gain
    ).astype(jnp.bfloat16)
    query_width = w_query.shape[1]
    kv_flat = w_kv.reshape(w_kv.shape[0], -1)
    whole = lax.all_gather(normed, "tp", axis=0, tiled=True)
    query = jnp.dot(
        whole,
        lax.all_gather(w_query, "req", axis=0, tiled=True),
        preferred_element_type=jnp.float32,
    )
    keyval = jnp.dot(
        whole,
        lax.all_gather(kv_flat, "req", axis=0, tiled=True),
        preferred_element_type=jnp.float32,
    )
    count = query.shape[0]
    local_heads = query_width // HD
    local_kv = kv_flat.shape[1] // (2 * HD)
    group = local_heads // local_kv
    seg_row = seg_ids[0]
    positions = segment_positions(seg_row)
    cosine, sine = rope_tables(positions, HD)
    q_normed = head_norm_rope(query.reshape(count, local_heads, HD), q_gain, cosine, sine)
    keyval = keyval.reshape(count, 2, local_kv, HD)
    k_normed = head_norm_rope(keyval[:, 0], k_gain, cosine, sine)
    v_round = keyval[:, 1].astype(jnp.bfloat16)
    pages_dev = page_table.shape[1]
    page_len = count // pages_dev
    devices = lax.axis_size("req")
    me = lax.axis_index("req")
    stacked = jnp.stack([k_normed, v_round], axis=1).reshape(
        pages_dev, page_len * 2 * local_kv * HD
    )
    my_row = lax.dynamic_slice_in_dim(page_table, me, 1, 0)[0]
    owners = my_row // pages_dev
    send_map = (owners[None, :] == jnp.arange(devices, dtype=jnp.int32)[:, None]).astype(
        jnp.bfloat16
    )
    outgoing = jnp.dot(send_map, stacked, preferred_element_type=jnp.float32).astype(jnp.bfloat16)
    incoming = lax.all_to_all(outgoing, "req", split_axis=0, concat_axis=0, tiled=True)
    targets = me * pages_dev + jnp.arange(pages_dev, dtype=jnp.int32)
    recv_map = jnp.any(page_table[None, :, :] == targets[:, None, None], axis=2).astype(
        jnp.bfloat16
    )
    cache = jnp.dot(recv_map, incoming, preferred_element_type=jnp.float32).astype(jnp.bfloat16)
    cache = cache.reshape(1, pages_dev, page_len, 2, local_kv * HD)
    grouped_q = q_normed.reshape(count, local_kv, group, HD)
    scale = HD ** (-0.5)
    index = jnp.arange(count, dtype=jnp.int32)
    scores = (
        jnp.einsum("qcgd,kcd->cgqk", grouped_q, k_normed, preferred_element_type=jnp.float32)
        * scale
    )
    allowed = (seg_row[:, None] == seg_row[None, :]) & (index[None, :] <= index[:, None])
    scores = jnp.where(allowed[None, None], scores, -1e30)
    probs = jax.nn.softmax(scores, axis=-1).astype(jnp.bfloat16)
    attended = jnp.einsum("cgqk,kcd->qcgd", probs, v_round, preferred_element_type=jnp.float32)
    attended = attended.reshape(count, local_heads * HD).astype(jnp.bfloat16)
    return (attended, cache)


MESH = pl.DeviceIdType.MESH
SIDE = 2
PLANE = SIDE * SIDE
PARTS = 4


def place():
    me = lax.axis_index("req")
    core = lax.axis_index("tp")
    z = me // PLANE
    q = me % PLANE
    across = q + 1 - 2 * (q % SIDE)
    along = (q + SIDE) % PLANE
    diagonal = PLANE - 1 - q
    return me, core, z, q, across, along, diagonal


def gather_kernel(depth, x_ref, w_ref, seg_ref, xs_ref, ws_ref, segs_ref,
                  xbuf, wbuf, sbuf, own_sem, w_send, w_recv, up_send, up_recv, down_send, down_recv,
                  x_send, x_recv, hop_send, hop_recv, near_send, near_recv, s_send, s_recv):
    me, core, z, q, across, along, diagonal = place()
    base = z * PLANE
    mates = (across, along, diagonal)
    barrier = pltpu.get_barrier_semaphore()
    for mate in mates:
        pl.semaphore_signal(barrier, inc=1, device_id=(base + mate, core), device_id_type=MESH)
    pl.semaphore_signal(barrier, inc=1, device_id=(me, 1 - core), device_id_type=MESH)

    @pl.when(z > 0)
    def _():
        pl.semaphore_signal(barrier, inc=1, device_id=(me - PLANE, core), device_id_type=MESH)

    @pl.when(z < depth - 1)
    def _():
        pl.semaphore_signal(barrier, inc=1, device_id=(me + PLANE, core), device_id_type=MESH)

    load_w = pltpu.make_async_copy(w_ref.at[q], wbuf, own_sem.at[0])
    load_x = pltpu.make_async_copy(x_ref, xbuf, own_sem.at[1])
    load_s = pltpu.make_async_copy(seg_ref, sbuf, own_sem.at[2])
    load_w.start()
    load_x.start()
    load_s.start()
    pl.semaphore_wait(barrier, len(mates) + 1 + (z > 0).astype(jnp.int32) + (z < depth - 1).astype(jnp.int32))
    rows = x_ref.shape[0] // PARTS

    def remote(source, target, send, receive, device):
        return pltpu.make_async_remote_copy(
            src_ref=source, dst_ref=target, send_sem=send, recv_sem=receive,
            device_id=device, device_id_type=MESH)

    def w_out(i):
        return remote(w_ref.at[mates[i]], ws_ref.at[z, q], w_send.at[i], w_recv.at[i], (base + mates[i], core))

    def w_in(i):
        return remote(w_ref.at[mates[i]], ws_ref.at[z, mates[i]], w_send.at[i], w_recv.at[i], (base + mates[i], core))

    def up(d, i, order):
        block = ws_ref.at[jnp.maximum(z - d, 0), order[i]]
        return remote(block, block, up_send.at[d, i], up_recv.at[d, i], (jnp.minimum(me + PLANE, depth * PLANE - 1), core))

    def down(d, i, order):
        block = ws_ref.at[jnp.minimum(z + d, depth - 1), order[i]]
        return remote(block, block, down_send.at[d, i], down_recv.at[d, i], (jnp.maximum(me - PLANE, 0), core))

    order = (q,) + mates

    def piece(owner, lane, k):
        return xs_ref.at[owner, lane, pl.ds(k * rows, rows)]

    def x_out(i, k):
        return remote(x_ref.at[pl.ds(k * rows, rows)], piece(q, core, k), x_send.at[i, k], x_recv.at[i, k], (base + mates[i], core))

    def x_in(i, k):
        return remote(x_ref.at[pl.ds(k * rows, rows)], piece(mates[i], core, k), x_send.at[i, k], x_recv.at[i, k], (base + mates[i], core))

    def hop(owner, k, target):
        return remote(piece(owner, core, k), piece(owner, core, k), hop_send.at[k], hop_recv.at[k], (base + target, core))

    def near(i, k):
        source = x_ref.at[pl.ds(k * rows, rows)] if i == 0 else piece(order[i], core, k)
        return remote(source, piece(order[i], core, k), near_send.at[i, k], near_recv.at[i, k], (me, 1 - core))

    def near_in(i, k):
        block = piece(order[i], 1 - core, k)
        return remote(block, block, near_send.at[i, k], near_recv.at[i, k], (me, 1 - core))

    def s_out(i):
        return remote(seg_ref, segs_ref.at[q], s_send.at[i], s_recv.at[i], (base + mates[i], core))

    def s_in(i):
        return remote(seg_ref, segs_ref.at[mates[i]], s_send.at[i], s_recv.at[i], (base + mates[i], core))

    for i in (2, 0, 1):
        w_out(i).start()
    for i in range(3):
        s_out(i).start()
    for k in range(PARTS):
        x_out(0, k).start()
        x_out(1, k).start()
    load_w.wait()
    save_w = pltpu.make_async_copy(wbuf, ws_ref.at[z, q], own_sem.at[0])
    save_w.start()
    load_s.wait()
    save_s = pltpu.make_async_copy(sbuf, segs_ref.at[q], own_sem.at[2])
    save_s.start()
    load_x.wait()
    save_x = pltpu.make_async_copy(xbuf, xs_ref.at[q, core], own_sem.at[1])
    save_x.start()
    save_w.wait()

    def push(d, i):
        @pl.when((z < depth - 1) & (z >= d))
        def _():
            up(d, i, order).start()

        @pl.when((z > 0) & (z + d < depth))
        def _():
            down(d, i, order).start()

    def arrive_up(d, i):
        block = ws_ref.at[jnp.maximum(z - d, 0), order[i]]
        remote(block, block, up_send.at[d - 1, i], up_recv.at[d - 1, i], (jnp.maximum(me - PLANE, 0), core)).wait_recv()

    def arrive_down(d, i):
        block = ws_ref.at[jnp.minimum(z + d, depth - 1), order[i]]
        remote(block, block, down_send.at[d - 1, i], down_recv.at[d - 1, i], (jnp.minimum(me + PLANE, depth * PLANE - 1), core)).wait_recv()

    def advance(d, i):
        @pl.when(z >= d)
        def _():
            arrive_up(d, i)
            if d < depth - 1:
                @pl.when(z < depth - 1)
                def _():
                    up(d, i, order).start()

        @pl.when(z + d < depth)
        def _():
            arrive_down(d, i)
            if d < depth - 1:
                @pl.when(z > 0)
                def _():
                    down(d, i, order).start()

    push(0, 0)
    for k in range(PARTS):
        near(0, k).start()
    for i in (0, 1, 2):
        w_in(i).wait_recv()
        push(0, i + 1)
    for k in range(PARTS):
        x_in(0, k).wait_recv()

        @pl.when(core == 0)
        def _():
            hop(across, k, along).start()

        near(1, k).start()
        x_in(1, k).wait_recv()

        @pl.when(core == 1)
        def _():
            hop(along, k, across).start()

        near(2, k).start()
        advance(1, k)
    for k in range(PARTS):
        advance(2, k)
        hop(diagonal, k, along).wait_recv()
        near(3, k).start()
    for i in range(PLANE):
        for d in range(3, depth):
            advance(d, i)
    for k in range(PARTS):
        for i in range(PLANE):
            near_in(i, k).wait_recv()
    for i in range(3):
        s_in(i).wait_recv()
        s_out(i).wait_send()
        w_out(i).wait_send()
    for k in range(PARTS):
        x_out(0, k).wait_send()
        x_out(1, k).wait_send()
        hop(across, k, along).wait_send()
        for i in range(PLANE):
            near(i, k).wait_send()
    for d in range(depth - 1):
        for i in range(PLANE):
            @pl.when((z < depth - 1) & (z >= d))
            def _():
                up(d, i, order).wait_send()

            @pl.when((z > 0) & (z + d < depth))
            def _():
                down(d, i, order).wait_send()
    save_x.wait()
    save_s.wait()


def gather(normed, blocks, seg, depth):
    rows, width = normed.shape
    dma = pltpu.SemaphoreType.DMA
    return pl.pallas_call(
        functools.partial(gather_kernel, depth),
        out_shape=(
            jax.ShapeDtypeStruct((PLANE, 2, rows, width), normed.dtype),
            jax.ShapeDtypeStruct((depth,) + blocks.shape, blocks.dtype),
            jax.ShapeDtypeStruct((PLANE,) + seg.shape, seg.dtype),
        ),
        in_specs=[pl.BlockSpec(memory_space=pl.ANY)] * 3,
        out_specs=(pl.BlockSpec(memory_space=pl.ANY),) * 3,
        scratch_shapes=[
            pltpu.VMEM(normed.shape, normed.dtype),
            pltpu.VMEM(blocks.shape[1:], blocks.dtype),
            pltpu.VMEM(seg.shape, seg.dtype),
            dma((3,)), dma((3,)), dma((3,)),
            dma((depth - 1, PLANE)), dma((depth - 1, PLANE)), dma((depth - 1, PLANE)), dma((depth - 1, PLANE)),
            dma((2, PARTS)), dma((2, PARTS)), dma((PARTS,)), dma((PARTS,)),
            dma((PLANE, PARTS)), dma((PLANE, PARTS)), dma((3,)), dma((3,)),
        ],
        compiler_params=pltpu.CompilerParams(collective_id=0, has_side_effects=True),
    )(normed, blocks, seg)


def return_kernel(total, att_ref, page_ref, out_ref, in_ref, abuf, pbuf, own_sem, a_send, a_recv, p_send, p_recv):
    me, core, z, q, across, along, diagonal = place()
    base = z * PLANE
    mates = (across, along, diagonal)
    barrier = pltpu.get_barrier_semaphore()
    for d in range(1, total):
        pl.semaphore_signal(barrier, inc=1, device_id=((me + d) % total, core), device_id_type=MESH)
    load_a = pltpu.make_async_copy(att_ref.at[q], abuf, own_sem.at[0])
    load_p = pltpu.make_async_copy(page_ref.at[me], pbuf, own_sem.at[1])
    load_a.start()
    load_p.start()
    pl.semaphore_wait(barrier, total - 1)
    width = att_ref.shape[2]

    def columns(owner):
        return out_ref.at[:, pl.ds(pl.multiple_of(owner * width, 128), width)]

    def a_copy(i, owner):
        return pltpu.make_async_remote_copy(
            src_ref=att_ref.at[mates[i]], dst_ref=columns(owner), send_sem=a_send.at[i], recv_sem=a_recv.at[i],
            device_id=(base + mates[i], core), device_id_type=MESH)

    def p_copy(d, slot, target):
        return pltpu.make_async_remote_copy(
            src_ref=page_ref.at[target], dst_ref=in_ref.at[slot], send_sem=p_send.at[d - 1], recv_sem=p_recv.at[d - 1],
            device_id=(target, core), device_id_type=MESH)

    far = [d for d in range(1, total)]
    for d in far:
        p_copy(d, me, (me + d) % total).start()
    for i in (2, 0, 1):
        a_copy(i, q).start()
    load_a.wait()
    load_p.wait()
    save_a = pltpu.make_async_copy(abuf, columns(q), own_sem.at[0])
    save_p = pltpu.make_async_copy(pbuf, in_ref.at[me], own_sem.at[1])
    save_a.start()
    save_p.start()
    for i in range(3):
        a_copy(i, mates[i]).wait_recv()
        a_copy(i, q).wait_send()
    for d in far:
        p_copy(d, (me + total - d) % total, (me + d) % total).wait_recv()
        p_copy(d, me, (me + d) % total).wait_send()
    save_a.wait()
    save_p.wait()


def give_back(attended, pages):
    total = pages.shape[0]
    dma = pltpu.SemaphoreType.DMA
    packs, count, width = attended.shape
    return pl.pallas_call(
        functools.partial(return_kernel, total),
        out_shape=(
            jax.ShapeDtypeStruct((count, packs * width), attended.dtype),
            jax.ShapeDtypeStruct(pages.shape, pages.dtype),
        ),
        in_specs=[pl.BlockSpec(memory_space=pl.ANY)] * 2,
        out_specs=(pl.BlockSpec(memory_space=pl.ANY),) * 2,
        scratch_shapes=[
            pltpu.VMEM(attended.shape[1:], attended.dtype),
            pltpu.VMEM(pages.shape[1:], pages.dtype),
            dma((2,)), dma((3,)), dma((3,)), dma((total - 1,)), dma((total - 1,)),
        ],
        compiler_params=pltpu.CompilerParams(collective_id=1, has_side_effects=True),
    )(attended, pages)


def attend_kernel(table_ref, x_ref, w_ref, seg_ref, q_gain_ref, k_gain_ref, index_ref, att_ref, out_ref, split, kv):
    pack = pl.program_id(0)
    count = seg_ref.shape[2]
    group = q_gain_ref.shape[0]
    f32, bf16 = jnp.float32, jnp.bfloat16

    @pl.when(pack == 0)
    def _():
        rest = table_ref[...]
        for i in range(3):
            part = rest.astype(bf16)
            split[:, i * HD : (i + 1) * HD] = part
            rest = rest - part.astype(f32)

    everything = jnp.dot(x_ref[0].reshape(count, -1), w_ref[...], preferred_element_type=f32)
    row = seg_ref[0]
    column = jnp.broadcast_to(row.astype(f32), (HD, count)).T[:, :1].astype(jnp.int32)
    before = jnp.sum((row < column).astype(f32), axis=1, keepdims=True).astype(jnp.int32)
    i = lax.broadcasted_iota(jnp.int32, (count, count), 0)
    j = lax.broadcasted_iota(jnp.int32, (count, count), 1)
    hot = (j == i - before).astype(f32).astype(bf16)
    allowed = (row == column) & (j <= i)
    parts = jnp.dot(hot, split[...], preferred_element_type=f32)
    both = parts[:, :HD] + parts[:, HD : 2 * HD] + parts[:, 2 * HD :]
    swapped = pltpu.roll(both, HD // 2, 1)
    low = lax.broadcasted_iota(jnp.int32, (count, HD), 1) < HD // 2
    cosine = jnp.where(low, both, swapped)
    sine = jnp.where(low, -swapped, both)

    def turn(values, gain):
        scaled = values * lax.rsqrt(jnp.mean(values * values, axis=1, keepdims=True) + 1e-06) * gain
        return (scaled * cosine + pltpu.roll(scaled, HD // 2, 1) * sine).astype(bf16)

    kn = turn(everything[:, group * HD : (group + 1) * HD], k_gain_ref[...])
    vv = everything[:, (group + 1) * HD :].astype(bf16)
    pages, page_len = kv.shape[0], kv.shape[1]
    kv[:, :, :HD] = kn.reshape(pages, page_len, HD)
    kv[:, :, HD:] = vv.reshape(pages, page_len, HD)

    def one(o, carry):
        out_ref[o, 0] = kv[index_ref[o, pack]]
        return carry

    lax.fori_loop(0, out_ref.shape[0], one, 0)
    half = count // 2
    for h in range(group):
        qn = turn(everything[:, h * HD : (h + 1) * HD], q_gain_ref[h : h + 1])
        for t in range(2):
            top, end = t * half, (t + 1) * half
            scores = lax.dot_general(
                qn[top:end], kn[:end], (((1,), (1,)), ((), ())), preferred_element_type=f32
            ) * HD ** (-0.5)
            scores = jnp.where(allowed[top:end, :end], scores, -1e30)
            weights = jnp.exp(scores - jnp.max(scores, axis=1, keepdims=True))
            probs = (weights / jnp.sum(weights, axis=1, keepdims=True)).astype(bf16)
            att_ref[0, top:end, h * HD : (h + 1) * HD] = jnp.dot(
                probs, vv[:end], preferred_element_type=f32
            ).astype(bf16)


def attend(table, xs, ws, segs, q_gain, k_gain, index, group, pages):
    packs, lanes, rows, width = xs.shape
    count = lanes * rows
    owners = index.shape[0]
    page_len = count // pages
    whole = lambda *shape: pl.BlockSpec(shape, lambda p: (0,) * len(shape))
    return pl.pallas_call(
        attend_kernel,
        grid=(packs,),
        out_shape=(
            jax.ShapeDtypeStruct((packs, count, group * HD), xs.dtype),
            jax.ShapeDtypeStruct((owners, packs, page_len, 2 * HD), xs.dtype),
        ),
        in_specs=[
            whole(*table.shape),
            pl.BlockSpec((1, lanes, rows, width), lambda p: (p, 0, 0, 0)),
            whole(*ws.shape),
            pl.BlockSpec((1, 1, count), lambda p: (p, 0, 0)),
            whole(group, HD),
            whole(1, HD),
            pl.BlockSpec(memory_space=pltpu.SMEM),
        ],
        out_specs=(
            pl.BlockSpec((1, count, group * HD), lambda p: (p, 0, 0)),
            pl.BlockSpec((owners, 1, page_len, 2 * HD), lambda p: (0, p, 0, 0)),
        ),
        scratch_shapes=[
            pltpu.VMEM((table.shape[0], 3 * HD), jnp.bfloat16),
            pltpu.VMEM((pages, page_len, 2 * HD), jnp.bfloat16),
        ],
    )(table, xs, ws, segs, jnp.broadcast_to(q_gain[None], (group, HD)), k_gain[None], index)


def plane_body(tokens, norm_gain, w_query, w_kv, q_gain, k_gain, seg_ids, page_table):
    me = lax.axis_index("req")
    devices = lax.axis_size("req")
    depth = devices // PLANE
    z = me // PLANE
    values_in = tokens.astype(jnp.float32)
    normed = (
        values_in
        * lax.rsqrt(jnp.mean(values_in * values_in, axis=1, keepdims=True) + 1e-06)
        * norm_gain
    ).astype(jnp.bfloat16)
    inner = w_query.shape[0]
    q_width = w_query.shape[1] // PLANE
    group = q_width // HD
    blocks = jnp.concatenate(
        [
            w_query.reshape(inner, PLANE, q_width),
            w_kv[:, 0].reshape(inner, PLANE, HD),
            w_kv[:, 1].reshape(inner, PLANE, HD),
        ],
        axis=2,
    ).transpose(1, 0, 2)
    count = seg_ids.shape[1]
    pages_dev = page_table.shape[1]
    rows = lax.dynamic_slice_in_dim(page_table, z * PLANE, PLANE, 0) // pages_dev
    match = rows[None, :, :] == jnp.arange(devices, dtype=jnp.int32)[:, None, None]
    index = jnp.sum(match * jnp.arange(pages_dev, dtype=jnp.int32), axis=2)
    cosine, sine = rope_tables(jnp.arange(count, dtype=jnp.int32), HD)
    table = jnp.concatenate([cosine[:, : HD // 2], sine[:, : HD // 2]], axis=1)
    xs, ws, segs = gather(normed, blocks, seg_ids.reshape(-1, HD), depth)
    attended, outgoing = attend(
        table, xs, ws.reshape(devices * inner, -1), segs.reshape(PLANE, 1, count),
        q_gain, k_gain, index, group, pages_dev,
    )
    attended, incoming = give_back(attended, outgoing)
    targets = me * pages_dev + jnp.arange(pages_dev, dtype=jnp.int32)
    found = jnp.any(page_table[None, :, :] == targets[:, None, None], axis=2)
    source = jnp.sum(found * jnp.arange(devices, dtype=jnp.int32), axis=1)
    cache = collect(source, incoming)
    return (attended, cache[None])


def collect_kernel(source_ref, in_ref, out_ref):
    slots = out_ref.shape[0]
    for s in range(slots):
        r = source_ref[s]
        for h in range(PLANE):
            page = in_ref[(r // PLANE) * PLANE + h, r % PLANE]
            for half in range(2):
                out_ref[s, :, half, h * HD : (h + 1) * HD] = page[:, half * HD : (half + 1) * HD]


def collect(source, incoming):
    slots = source.shape[0]
    rows = incoming.shape[2]
    return pl.pallas_call(
        collect_kernel,
        out_shape=jax.ShapeDtypeStruct((slots, rows, 2, PLANE * HD), incoming.dtype),
        in_specs=[pl.BlockSpec(memory_space=pltpu.SMEM), pl.BlockSpec(memory_space=pltpu.VMEM)],
        out_specs=pl.BlockSpec(memory_space=pltpu.VMEM),
    )(source, incoming)


def solution(mesh):
    placed = (
        P(("req", "tp"), None),
        P(),
        P("req", "tp"),
        P("req", None, "tp"),
        P(),
        P(),
        P("req", None),
        P(),
    )
    planes = mesh.shape["req"] == 4 * PLANE and mesh.shape["tp"] == 2
    return jax.shard_map(
        plane_body if planes else body,
        mesh=mesh,
        in_specs=placed,
        out_specs=(P("req", "tp"), P("req", None, None, None, "tp")),
        check_vma=False,
    )
```
